32 devices in a mesh: expert: 4 (over y, core), replica: 2 (over x), seq: 4 (over z).
Axes of the slice: x: 2, y: 2, z: 4, core: 2. Of those that a mesh axis runs over, the one named last changes fastest.
Arguments:
- tokens: bfloat16 [1536, 3584], P(('expert', 'replica'), 'seq'), may hold values from -6 to 6
- cotangent: bfloat16 [1536, 3584], P(('expert', 'replica'), 'seq'), may hold values from -6 to 6
- route_weight: float32 [1536], P(('expert', 'replica')), may hold values from 0.1 to 1
- expert_ids: int32 [1536, 1], P(('expert', 'replica')), may hold values from 0 to 3; in each aligned block of 192 rows (0 to 191, 192 to 383, ...) at most 72 rows name the same one
- gate_weight: bfloat16 [4, 3584, 1024], P('expert', 'seq', 'replica'), may hold values from -0.09375 to 0.09375
- up_weight: bfloat16 [4, 3584, 1024], P('expert', 'seq', 'replica'), may hold values from -0.09375 to 0.09375
- down_weight: bfloat16 [4, 1024, 3584], P('expert', 'replica', 'seq'), may hold values from -0.1875 to 0.1875
Outputs:
- token_grad: bfloat16 [1536, 3584], P(('expert', 'replica'), 'seq')
- gate_grad: bfloat16 [4, 3584, 1024], P('expert', 'seq', 'replica')
- up_grad: bfloat16 [4, 3584, 1024], P('expert', 'seq', 'replica')
- down_grad: bfloat16 [4, 1024, 3584], P('expert', 'replica', 'seq')
The draws below stay inside these ranges and needn't reach their ends.
Inputs may be any that keep to these rules, and one draw needn't show every extreme that they name: `expert_ids`: among the 192 tokens of one block (the tokens of one device) no expert is named more than 72 times, a bound that some block reaches.
All inputs are finite; a program needn't handle non-finite values.
Results may differ from the reference program's by a relative error of at most 0.02.
Values may be sent and summed in bfloat16 or wider, within the bound.
No kernel may reach another device: no remote copies, remote signals or barrier semaphores. Data moves between devices by JAX's collectives and lax.ppermute only.
A program may use at most 64 MiB of HBM per device.

```python
import math
import jax
import jax.numpy as jnp
import numpy as np
from jax import lax

D = 3584
F = 1024
TOPK = 1
TOK_DEV = 192
EXPERTS = 4
CAP = 72
TOKENS = 1536
N_REPLICA = 2
N_SEQ = 4


def block_levels(own_key, dims, shards, least, top_value):
    gain = 1.0
    for axis_at, blocks in shards:
        heights = jax.random.uniform(jax.random.fold_in(jax.random.fold_in(own_key, 6), axis_at), (blocks,), jnp.float32, least / len(shards), top_value / len(shards))
        gain = gain * jnp.repeat(jnp.exp(heights), dims[axis_at] // blocks).reshape((-1,) + (1,) * (len(dims) - 1 - axis_at))
    return gain


def shared_out(rng, own, number, rows, count, top, bound, skew):
    ranking = jax.random.permutation(rng, count)
    heavy_load, ordinary = portions_of(count, rows * top, bound, skew, True), portions_of(count, rows * top, bound, skew, False)
    places = jnp.arange(count)

    def named(tallies, turn):
        used = int((tallies > 0).sum())
        fixed = max(1, used // 4)
        moved = fixed + (places - fixed + turn * (used - fixed)) % max(1, count - fixed)
        return jnp.zeros((count,), jnp.int32).at[ranking[jnp.where(places < fixed, places, moved)]].set(jnp.asarray(tallies, jnp.int32))

    tallies = jnp.where(number % 4 == 0, named(heavy_load, number // 4), named(ordinary, number - number // 4 - 1))
    mixed = jax.random.permutation(jax.random.fold_in(own, 3), count)
    giver, receiver = mixed[0:count // 2 * 2:2], mixed[1:count // 2 * 2:2]
    room = jnp.minimum(tallies[giver] - 1, bound - tallies[receiver]) // 2
    room = jnp.where((giver == ranking[0]) | (receiver == ranking[0]) | (tallies[receiver] == 0), 0, jnp.maximum(room, 0))
    moved = jax.random.randint(jax.random.fold_in(own, 4), (count // 2,), 0, 1 << 20) % (room + 1)
    tallies = tallies.at[giver].add(-moved).at[receiver].add(moved)
    members = jnp.searchsorted(jnp.cumsum(tallies), jnp.arange(rows * top), side="right").astype(jnp.int32)
    table = members.reshape(top, rows).T
    table = table[jax.random.permutation(jax.random.fold_in(own, 1), rows)]
    turn = jax.random.randint(jax.random.fold_in(own, 2), (rows, 1), 0, top)
    return jnp.take_along_axis(table, (jnp.arange(top)[None, :] + turn) % top, axis=1)


def portions_of(number_of, total, reach, lean, full):
    weights = [(1 << 20) // math.isqrt(grade ** lean) + 1 for grade in range(1, number_of + 1)]
    largest = reach if full else min(reach, max(-(-total // number_of), total * weights[0] // sum(weights)))
    least = 1 if total - largest >= number_of - 1 else 0
    holding, surplus = [largest] + [least] * (number_of - 1), total - largest - least * (number_of - 1)
    while surplus > 0:
        movable = [i for i in range(1, number_of) if holding[i] < largest] or [i for i in range(1, number_of) if holding[i] < reach]
        mass, budget = sum([weights[i] for i in movable]), surplus
        for i in movable:
            more = min(reach - holding[i], max(1, budget * weights[i] // mass), surplus)
            holding[i] = holding[i] + more
            surplus = surplus - more
    return np.array(holding)


def scatter_about(stream_key, extent, scale, limit, shards=(), kind=jnp.bfloat16):
    values = scale * jax.random.normal(stream_key, extent, jnp.float32)
    if shards:
        values = values * block_levels(stream_key, extent, shards, -0.22, 0.18)
    return jnp.clip(values, -limit, limit).astype(kind)


def setup_inputs(seed: int = 0) -> dict:
    seeds = jax.random.split(jax.random.key(seed), 8)
    tokens = scatter_about(seeds[0], (TOKENS, D), 1.0, 6.0, ((0, 8), (1, 4)))
    cotangent = scatter_about(seeds[1], (TOKENS, D), 1.0, 6.0, ((0, 8), (1, 4)))
    route_weight = jnp.clip(jnp.exp(math.log(1.0) - 2.3025851 * jax.random.uniform(seeds[2], (TOKENS,), jnp.float32) ** block_levels(seeds[2], (TOKENS,), ((0, 8),), -0.2, 0.2)), 0.1, 1.0)
    expert_ids_keys = jax.random.split(jax.random.fold_in(seeds[3], 1), TOKENS // TOK_DEV)
    expert_ids_turns = jax.random.permutation(jax.random.fold_in(seeds[3], 3), TOKENS // TOK_DEV)
    expert_ids = jax.vmap(lambda own, number: shared_out(jax.random.fold_in(seeds[3], 2), own, number, TOK_DEV, EXPERTS, TOPK, CAP, 2))(expert_ids_keys, expert_ids_turns).reshape((TOKENS, TOPK))
    gate_weight = scatter_about(seeds[4], (EXPERTS, D, F), D ** -0.5, 0.09375, ((0, 4), (1, 4), (2, 2)))
    up_weight = scatter_about(seeds[5], (EXPERTS, D, F), D ** -0.5, 0.09375, ((0, 4), (1, 4), (2, 2)))
    down_weight = scatter_about(seeds[6], (EXPERTS, F, D), F ** -0.5, 0.1875, ((0, 4), (1, 2), (2, 4)))
    return {"tokens": tokens, "cotangent": cotangent, "route_weight": route_weight, "expert_ids": expert_ids, "gate_weight": gate_weight, "up_weight": up_weight, "down_weight": down_weight}


def reference(tokens, cotangent, route_weight, expert_ids, gate_weight, up_weight, down_weight):
    blocks = TOKENS // TOK_DEV
    quarter = D // N_SEQ
    chosen = expert_ids[:, 0].reshape(blocks, TOK_DEV)
    onehot = (chosen[:, :, None] == jnp.arange(EXPERTS, dtype=jnp.int32)[None, None, :]).astype(jnp.int32)
    before = jnp.cumsum(onehot, axis=1) - onehot
    within = jnp.sum(before * onehot, axis=2)
    target = chosen * CAP + within
    local_rows = (jnp.arange(TOK_DEV, dtype=jnp.int32)[None, :] + TOK_DEV * jnp.arange(blocks, dtype=jnp.int32)[:, None]).astype(jnp.int32)
    block_ids = jnp.broadcast_to(jnp.arange(blocks, dtype=jnp.int32)[:, None], (blocks, TOK_DEV))
    table = jnp.full((blocks, EXPERTS * CAP), TOKENS, jnp.int32).at[block_ids, target].set(local_rows)
    table = table.reshape(blocks, EXPERTS, CAP)
    padded_x = jnp.concatenate([tokens, jnp.zeros((1, D), jnp.bfloat16)], axis=0)
    scaled = (route_weight[:, None] * cotangent.astype(jnp.float32)).astype(jnp.bfloat16)
    padded_g = jnp.concatenate([scaled, jnp.zeros((1, D), jnp.bfloat16)], axis=0)

    def expert_step(carry, index):
        picked = table[:, index, :].reshape(-1)
        x_rows = padded_x[picked]
        g_rows = padded_g[picked]
        w_gate = gate_weight[index]
        w_up = up_weight[index]
        w_down = down_weight[index]
        x_quart = x_rows.astype(jnp.float32).reshape(-1, N_SEQ, quarter)
        g_quart = g_rows.astype(jnp.float32).reshape(-1, N_SEQ, quarter)
        part_gate = jnp.einsum('rqd,qdf->rqf', x_quart, w_gate.astype(jnp.float32).reshape(N_SEQ, quarter, F))
        part_up = jnp.einsum('rqd,qdf->rqf', x_quart, w_up.astype(jnp.float32).reshape(N_SEQ, quarter, F))
        part_dh = jnp.einsum('rqd,fqd->rqf', g_quart, w_down.astype(jnp.float32).reshape(F, N_SEQ, quarter))
        gate = jnp.sum(part_gate.astype(jnp.bfloat16).astype(jnp.float32), axis=1)
        upper = jnp.sum(part_up.astype(jnp.bfloat16).astype(jnp.float32), axis=1)
        hgrad = jnp.sum(part_dh.astype(jnp.bfloat16).astype(jnp.float32), axis=1)
        sigma = jax.nn.sigmoid(gate)
        active = gate * sigma
        hidden = (active * upper).astype(jnp.bfloat16)
        gate_delta = (hgrad * upper * sigma * (1.0 + gate * (1.0 - sigma))).astype(jnp.bfloat16)
        up_delta = (hgrad * active).astype(jnp.bfloat16)
        out_rows = (jnp.dot(gate_delta, w_gate.T, preferred_element_type=jnp.float32)
                    + jnp.dot(up_delta, w_up.T, preferred_element_type=jnp.float32)).astype(jnp.bfloat16)
        carry = carry.at[picked].set(out_rows)
        groups = blocks // N_REPLICA
        x_grp = x_rows.astype(jnp.float32).reshape(groups, N_REPLICA, CAP, D)
        g_grp = g_rows.astype(jnp.float32).reshape(groups, N_REPLICA, CAP, D)
        h_grp = hidden.astype(jnp.float32).reshape(groups, N_REPLICA, CAP, F)
        dg_grp = gate_delta.astype(jnp.float32).reshape(groups, N_REPLICA, CAP, F)
        du_grp = up_delta.astype(jnp.float32).reshape(groups, N_REPLICA, CAP, F)
        grad_gate = jnp.einsum('brcd,brcf->rdf', x_grp, dg_grp).astype(jnp.bfloat16).astype(jnp.float32)
        grad_up = jnp.einsum('brcd,brcf->rdf', x_grp, du_grp).astype(jnp.bfloat16).astype(jnp.float32)
        grad_down = jnp.einsum('brcf,brcd->rfd', h_grp, g_grp).astype(jnp.bfloat16).astype(jnp.float32)
        return carry, (jnp.sum(grad_gate, axis=0).astype(jnp.bfloat16),
                       jnp.sum(grad_up, axis=0).astype(jnp.bfloat16),
                       jnp.sum(grad_down, axis=0).astype(jnp.bfloat16))

    start = jnp.zeros((TOKENS + 1, D), jnp.bfloat16)
    back, grads = lax.scan(expert_step, start, jnp.arange(EXPERTS, dtype=jnp.int32))
    token_grad = (route_weight[:, None] * back[:TOKENS].astype(jnp.float32)).astype(jnp.bfloat16)
    return token_grad, grads[0], grads[1], grads[2]
```

```python
import functools

import jax
import jax.numpy as jnp
from jax import lax
from jax.experimental import pallas as pl
from jax.experimental.pallas import tpu as pltpu
from jax.sharding import PartitionSpec as P

F32 = jnp.float32
BF16 = jnp.bfloat16
VMEM = pltpu.VMEM
SMEM = pltpu.SMEM


def mm(left, right, dims):
    return lax.dot_general(left, right, (dims, ((), ())), preferred_element_type=F32)


NN = ((1,), (0,))
NT = ((1,), (1,))
TN = ((0,), (0,))


def call(body, out_shape, n_smem, n_vmem, name, scratch=()):
    outs = out_shape if isinstance(out_shape, (list, tuple)) else [out_shape]
    return pl.pallas_call(
        body,
        out_shape=out_shape,
        in_specs=[pl.BlockSpec(memory_space=SMEM)] * n_smem + [pl.BlockSpec(memory_space=VMEM)] * n_vmem,
        out_specs=jax.tree.map(lambda _: pl.BlockSpec(memory_space=VMEM), out_shape),
        scratch_shapes=list(scratch),
        name=name,
    )


def column(row):
    count = row.shape[1]
    eye = lax.broadcasted_iota(jnp.int32, (count, count), 0) == lax.broadcasted_iota(jnp.int32, (count, count), 1)
    return jnp.sum(jnp.where(eye, row, jnp.zeros_like(row)), axis=1, keepdims=True)


def slots(ids, rank, owner, cap):
    places = lax.broadcasted_iota(jnp.int32, (ids.shape[0], cap), 1)
    return jnp.where((ids == owner) & (rank == places), 1.0, 0.0).astype(BF16)


def prep_body(n_expert, cap, ids_ref, tokens_ref, cot_ref, rw_ref, sx_ref, sg_ref, rank_ref):
    ids = ids_ref[...]
    count = ids.shape[0]
    lanes = lax.broadcasted_iota(jnp.int32, (count, 128), 1)
    onehot = jnp.where(ids == lanes, 1.0, 0.0)
    lower = jnp.where(
        lax.broadcasted_iota(jnp.int32, (count, count), 0) > lax.broadcasted_iota(jnp.int32, (count, count), 1), 1.0, 0.0
    )
    before = mm(lower.astype(BF16), onehot.astype(BF16), NN)
    rank = jnp.sum(before * onehot, axis=1, keepdims=True).astype(jnp.int32)
    rank_ref[...] = rank
    tokens = tokens_ref[...]
    scaled = (column(rw_ref[...]) * cot_ref[...].astype(F32)).astype(BF16)
    for j in range(n_expert):
        pick = slots(ids, rank, j, cap)
        sx_ref[j] = mm(pick, tokens, TN).astype(BF16)
        sg_ref[j] = mm(pick, scaled, TN).astype(BF16)


def part_body(half, waves, x_ref, g_ref, wg_ref, wu_ref, wd_ref, *outs):
    x = x_ref[...]
    g = g_ref[...]
    pg = mm(x, wg_ref[...], NN).astype(BF16)
    pu = mm(x, wu_ref[...], NN).astype(BF16)
    pd = mm(g, wd_ref[...], NT).astype(BF16)
    rows = x.shape[0] // waves
    for i in range(waves):
        outs[i][:, :half] = pg[i * rows:(i + 1) * rows]
        outs[i][:, half:2 * half] = pu[i * rows:(i + 1) * rows]
        outs[i][:, 2 * half:] = pd[i * rows:(i + 1) * rows]


def act_body(half, s_ref, m_ref, o_ref):
    gate = s_ref[:, :half].astype(F32) + m_ref[:, :half].astype(F32)
    upper = s_ref[:, half:2 * half].astype(F32) + m_ref[:, half:2 * half].astype(F32)
    hgrad = s_ref[:, 2 * half:].astype(F32) + m_ref[:, 2 * half:].astype(F32)
    sigma = jax.nn.sigmoid(gate)
    active = gate * sigma
    o_ref[:, :half] = (hgrad * upper * sigma * (1.0 + gate * (1.0 - sigma))).astype(BF16)
    o_ref[:, half:2 * half] = (hgrad * active).astype(BF16)
    o_ref[:, 2 * half:] = (active * upper).astype(BF16)


def out_body(half, edge_ref, t_ref, r_ref, wg_ref, wu_ref, a_ref, o_ref):
    @pl.when(edge_ref[0] == 1)
    def _():
        a_ref[...] = r_ref[...]

    @pl.when(edge_ref[0] == 0)
    def _():
        a_ref[...] = t_ref[...]

    o_ref[...] = (
        mm(a_ref[:, :half], wg_ref[...], NT) + mm(a_ref[:, half:2 * half], wu_ref[...], NT)
    ).astype(BF16)


def wgrad_body(half, n_x, n_a, *refs):
    xs, gs, acts = refs[:n_x], refs[n_x:2 * n_x], refs[2 * n_x:2 * n_x + n_a]
    gg_ref, gu_ref, gd_ref = refs[2 * n_x + n_a:]
    x = jnp.concatenate([r[...] for r in xs], axis=0)
    g = jnp.concatenate([r[...] for r in gs], axis=0)
    a = jnp.concatenate([r[...] for r in acts], axis=0)
    gg_ref[0] = mm(x, a[:, :half], TN).astype(BF16)
    gu_ref[0] = mm(x, a[:, half:2 * half], TN).astype(BF16)
    gd_ref[0] = mm(a[:, 2 * half:], g, TN).astype(BF16)


def final_body(n_expert, cap, ids_ref, rank_ref, rw_ref, ret_ref, o_ref):
    ids = ids_ref[...]
    rank = rank_ref[...]
    total = None
    for j in range(n_expert):
        term = mm(slots(ids, rank, j, cap), ret_ref[j], NN)
        total = term if total is None else total + term
    o_ref[...] = (column(rw_ref[...]) * total).astype(BF16)


def local(tokens, cotangent, route_weight, expert_ids, gate_weight, up_weight, down_weight):
    n_expert = lax.axis_size("expert")
    n_rep = lax.axis_size("replica")
    n_seq = lax.axis_size("seq")
    assert n_seq == 4 and n_rep & (n_rep - 1) == 0
    count, quarter = tokens.shape
    half = gate_weight.shape[2]
    cap = -(-(3 * count // (2 * n_expert)) // 8) * 8
    rows = n_expert * cap
    waves = 2
    wrows = rows // waves
    sds = jax.ShapeDtypeStruct
    z = lax.axis_index("seq")
    is_edge = (z == 0) | (z == n_seq - 1)
    edge = is_edge.astype(jnp.int32).reshape(1)
    w_gate, w_up, w_down = gate_weight[0], up_weight[0], down_weight[0]
    rw = route_weight.reshape(1, count)

    send_x, send_g, rank = call(
        functools.partial(prep_body, n_expert, cap),
        [sds((n_expert, cap, quarter), BF16), sds((n_expert, cap, quarter), BF16), sds((count, 1), jnp.int32)],
        0, 4, "prep",
    )(expert_ids, tokens, cotangent, rw)
    own_x = lax.all_to_all(send_x, "expert", 0, 0, tiled=True).reshape(rows, quarter)
    own_g = lax.all_to_all(send_g, "expert", 0, 0, tiled=True).reshape(rows, quarter)
    xs, gs = [own_x], [own_g]
    for k in range(1, n_rep):
        pairs = [(i, i ^ k) for i in range(n_rep)]
        xs.append(lax.ppermute(own_x, "replica", pairs))
        gs.append(lax.ppermute(own_g, "replica", pairs))
    parts = []
    for k in range(n_rep):
        parts += call(
            functools.partial(part_body, half, waves), [sds((wrows, 3 * half), BF16)] * waves, 0, 5, f"part{k}"
        )(xs[k], gs[k], w_gate, w_up, w_down)

    n_wave = len(parts)
    lag = 3
    sums, acts, outs = {}, {}, {}
    full = []
    inward, outward, middle = [(0, 1), (3, 2)], [(1, 0), (2, 3)], [(1, 2), (2, 1)]
    act = call(functools.partial(act_body, half), sds((wrows, 3 * half), BF16), 0, 2, "act")
    out = call(
        functools.partial(out_body, half), [sds((wrows, 3 * half), BF16), sds((wrows, quarter), BF16)], 1, 4, "out"
    )
    for i in range(n_wave + lag):
        back = i - lag
        if back < 0:
            got = lax.ppermute(parts[i], "seq", inward)
        elif i < n_wave:
            got = lax.ppermute(jnp.where(is_edge, parts[i], acts[back]), "seq", inward + outward)
        else:
            got = lax.ppermute(acts[back], "seq", outward)
        if i < n_wave:
            sums[i] = (parts[i].astype(F32) + got.astype(F32)).astype(BF16)
            acts[i] = act(sums[i], lax.ppermute(sums[i], "seq", middle))
        if back >= 0:
            a, o = out(edge, acts[back], got, w_gate, w_up)
            full.append(a)
            outs[back] = o

    total = [outs[i].astype(F32) for i in range(waves)]
    for k in range(1, n_rep):
        pairs = [(i, i ^ k) for i in range(n_rep)]
        for i in range(waves):
            total[i] = total[i] + lax.ppermute(outs[k * waves + i], "replica", pairs).astype(F32)
    back_rows = jnp.concatenate([t.astype(BF16) for t in total], axis=0).reshape(n_expert, cap, quarter)
    returned = lax.all_to_all(back_rows, "expert", 0, 0, tiled=True)
    gate_grad, up_grad, down_grad = call(
        functools.partial(wgrad_body, half, n_rep, n_wave),
        [sds((1, quarter, half), BF16), sds((1, quarter, half), BF16), sds((1, half, quarter), BF16)],
        0, 2 * n_rep + n_wave, "wgrad",
    )(*xs, *gs, *full)
    token_grad = call(
        functools.partial(final_body, n_expert, cap), sds((count, quarter), BF16), 0, 4, "final"
    )(expert_ids, rank, rw, returned)
    return (token_grad, gate_grad, up_grad, down_grad)


def solution(mesh):
    placed = (
        P(("expert", "replica"), "seq"),
        P(("expert", "replica"), "seq"),
        P(("expert", "replica")),
        P(("expert", "replica"), None),
        P("expert", "seq", "replica"),
        P("expert", "seq", "replica"),
        P("expert", "replica", "seq"),
    )
    return jax.shard_map(
        local,
        mesh=mesh,
        in_specs=placed,
        out_specs=(
            P(("expert", "replica"), "seq"),
            P("expert", "seq", "replica"),
            P("expert", "seq", "replica"),
            P("expert", "replica", "seq"),
        ),
        check_vma=False,
    )
```

```python
import functools

import jax
import jax.numpy as jnp
from jax import lax
from jax.experimental import pallas as pl
from jax.experimental.pallas import tpu as pltpu
from jax.sharding import PartitionSpec as P


F32 = jnp.float32
BF16 = jnp.bfloat16
VMEM = pltpu.VMEM
SMEM = pltpu.SMEM


def mm(left, right, dims):
    return lax.dot_general(left, right, (dims, ((), ())), preferred_element_type=F32)


NN = ((1,), (0,))
NT = ((1,), (1,))
TN = ((0,), (0,))


def vm(x):
    return pltpu.with_memory_space_constraint(x, pltpu.VMEM)


def call(body, outs, n_smem, args, raw=()):
    return pl.pallas_call(
        body,
        out_shape=outs,
        in_specs=[pl.BlockSpec(memory_space=SMEM)] * n_smem + [pl.BlockSpec(memory_space=VMEM)] * (len(args) - n_smem),
        out_specs=jax.tree.map(lambda _: pl.BlockSpec(memory_space=VMEM), outs),
        compiler_params=pltpu.CompilerParams(vmem_limit_bytes=16 << 20),
    )(*args[:n_smem], *[a if i in raw else vm(a) for i, a in enumerate(args) if i >= n_smem])


def column(row):
    count = row.shape[1]
    eye = lax.broadcasted_iota(jnp.int32, (count, count), 0) == lax.broadcasted_iota(jnp.int32, (count, count), 1)
    return jnp.sum(jnp.where(eye, row, jnp.zeros_like(row)), axis=1, keepdims=True)


def ranks(ids):
    count = ids.shape[0]
    lanes = lax.broadcasted_iota(jnp.int32, (count, 128), 1)
    onehot = jnp.where(ids == lanes, 1.0, 0.0)
    lower = jnp.where(
        lax.broadcasted_iota(jnp.int32, (count, count), 0) > lax.broadcasted_iota(jnp.int32, (count, count), 1), 1.0, 0.0
    )
    before = mm(lower.astype(BF16), onehot.astype(BF16), NN)
    return jnp.sum(before * onehot, axis=1, keepdims=True).astype(jnp.int32)


def slots(ids, rank, owner, cap):
    places = lax.broadcasted_iota(jnp.int32, (ids.shape[0], cap), 1)
    return jnp.where((ids == owner) & (rank == places), 1.0, 0.0).astype(BF16)


def send_body(n_expert, cap, own_ref, ids_ref, rw_ref, tokens_ref, cot_ref, *outs):
    ids = column(ids_ref[...])
    rank = ranks(ids)
    tokens = tokens_ref[...]
    scaled = (column(rw_ref[...]) * cot_ref[...].astype(F32)).astype(BF16)
    for k in range(n_expert):
        pick = slots(ids, rank, own_ref[0] ^ k, cap)
        outs[k][0, 0] = mm(pick, tokens, TN).astype(BF16)
        outs[k][0, 1] = mm(pick, scaled, TN).astype(BF16)


def side(refs, which):
    return jnp.concatenate([r[j, which] for r in refs for j in range(r.shape[0])], axis=0)


def part_body(half, n, *refs):
    rows, (wg_ref, wu_ref, wd_ref), outs = refs[:n], refs[n:n + 3], refs[n + 3:]
    x, g = side(rows, 0), side(rows, 1)
    parts = (mm(x, wg_ref[...], NN), mm(x, wu_ref[...], NN), mm(g, wd_ref[...], NT))
    size = outs[0].shape[0]
    for i in range(n):
        for j in range(3):
            outs[i][:, j * half:(j + 1) * half] = parts[j][i * size:(i + 1) * size].astype(BF16)


def join_body(p_ref, c_ref, o_ref):
    o_ref[...] = (p_ref[...].astype(F32) + c_ref[...].astype(F32)).astype(BF16)


def act_body(half, s_ref, m_ref, o_ref):
    gate = s_ref[:, :half].astype(F32) + m_ref[:, :half].astype(F32)
    upper = s_ref[:, half:2 * half].astype(F32) + m_ref[:, half:2 * half].astype(F32)
    hgrad = s_ref[:, 2 * half:].astype(F32) + m_ref[:, 2 * half:].astype(F32)
    sigma = jax.nn.sigmoid(gate)
    active = gate * sigma
    o_ref[:, :half] = (hgrad * upper * sigma * (1.0 + gate * (1.0 - sigma))).astype(BF16)
    o_ref[:, half:2 * half] = (hgrad * active).astype(BF16)
    o_ref[:, 2 * half:] = (active * upper).astype(BF16)


def out_body(half, n, *refs):
    acts, (wg_ref, wu_ref, o_ref) = refs[:n], refs[n:]
    a = jnp.concatenate([r[:, :2 * half] for r in acts], axis=0)
    o_ref[...] = (mm(a[:, :half], wg_ref[...], NT) + mm(a[:, half:], wu_ref[...], NT)).astype(BF16)


def wgrad_body(half, n, *refs):
    rows, acts, (gg_ref, gu_ref, gd_ref) = refs[:n], refs[n:2 * n], refs[2 * n:]
    x, g = side(rows, 0), side(rows, 1)
    a = jnp.concatenate([r[...] for r in acts], axis=0)
    gg_ref[0] = mm(x, a[:, :half], TN).astype(BF16)
    gu_ref[0] = mm(x, a[:, half:2 * half], TN).astype(BF16)
    gd_ref[0] = mm(a[:, 2 * half:], g, TN).astype(BF16)


def final_body(n_expert, cap, own_ref, ids_ref, rw_ref, *refs):
    ids = column(ids_ref[...])
    rank = ranks(ids)
    total = None
    for k in range(n_expert):
        term = mm(slots(ids, rank, own_ref[0] ^ k, cap), refs[k][...], NN)
        total = term if total is None else total + term
    refs[n_expert][...] = (column(rw_ref[...]) * total).astype(BF16)


def steps(tokens, cotangent, route_weight, expert_ids, gate_weight, up_weight, down_weight):
    n_expert = lax.axis_size("expert")
    n_rep = lax.axis_size("replica")
    n_seq = lax.axis_size("seq")
    assert n_seq == 4 and n_expert % 4 == 0
    count, quarter = tokens.shape
    half = gate_weight.shape[2]
    cap = -(-(3 * count // (2 * n_expert)) // 8) * 8
    each = n_expert // 4
    z = lax.axis_index("seq")
    is_edge = (z == 0) | (z == n_seq - 1)
    own = lax.axis_index("expert").reshape(1)
    w_gate, w_up, w_down = gate_weight[0], up_weight[0], down_weight[0]
    rw = route_weight.reshape(1, count)
    ids = expert_ids.reshape(1, count)
    keep = lambda *shape: pltpu.VMEM(shape, BF16)

    def swap(x, axis, k):
        return lax.ppermute(x, axis, [(i, i ^ k) for i in range(lax.axis_size(axis))])

    send = call(
        functools.partial(send_body, n_expert, cap), [keep(1, 2, cap, quarter)] * n_expert, 1,
        (own, ids, rw, tokens, cotangent), (1, 2, 3, 4),
    )
    got = [send[0]] + [swap(send[k], "expert", k) for k in range(1, n_expert)]
    rows = {}
    for j in range(4):
        blocks = got[j * each:(j + 1) * each]
        rows[0, j] = blocks[0] if each == 1 else jnp.concatenate(blocks, axis=0)
    for q in range(1, n_rep):
        for j in range(4):
            rows[q, j] = swap(rows[0, j], "replica", q)
    size = each * cap
    parts = {}
    for q in range(n_rep):
        for pair in ((0, 1), (2, 3)):
            done = call(
                functools.partial(part_body, half, 2), [keep(size, 3 * half)] * 2, 0,
                (*[rows[q, j] for j in pair], w_gate, w_up, w_down),
                (2, 3, 4) if (q, pair) == (0, (0, 1)) else (),
            )
            parts[q, pair[0]], parts[q, pair[1]] = done

    waves = [(0, 1), (0, 2), (0, 3)]
    waves += [(q, j) for q in range(1, n_rep) for j in (0, 2, 3, 1)] + [(0, 0)]
    lag = 3
    inward, outward, middle = [(0, 1), (3, 2)], [(1, 0), (2, 3)], [(1, 2), (2, 1)]
    acts, full = {}, {}
    for i in range(len(waves) + lag):
        now = waves[i] if i < len(waves) else None
        old = waves[i - lag] if i >= lag else None
        if old is None:
            came = lax.ppermute(parts[now], "seq", inward)
        elif now is None:
            came = lax.ppermute(acts[old], "seq", outward)
        else:
            came = lax.ppermute(jnp.where(is_edge, parts[now], acts[old]), "seq", inward + outward)
        if now is not None:
            pair = call(join_body, keep(size, 3 * half), 0, (parts[now], came))
            acts[now] = call(
                functools.partial(act_body, half), keep(size, 3 * half), 0,
                (pair, lax.ppermute(pair, "seq", middle)),
            )
        if old is not None:
            full[old] = jnp.where(is_edge, came, acts[old])

    def out(q, pair):
        return call(
            functools.partial(out_body, half, 2), keep(2 * size, quarter), 0,
            (*[full[q, j] for j in pair], w_gate, w_up),
        )

    high, low = out(0, (2, 3)).astype(F32), None
    for q in range(1, n_rep):
        high = high + swap(out(q, (2, 3)), "replica", q).astype(F32)
    low = out(0, (0, 1)).astype(F32)
    for q in range(1, n_rep):
        low = low + swap(out(q, (0, 1)), "replica", q).astype(F32)
    total = [t[k * cap:(k + 1) * cap].astype(BF16) for t in (low, high) for k in range(2 * each)]
    ret = [total[0]] + [swap(total[k], "expert", k) for k in range(1, n_expert)]
    sds = jax.ShapeDtypeStruct
    token_grad = call(
        functools.partial(final_body, n_expert, cap), sds((count, quarter), BF16), 1, (own, ids, rw, *ret)
    )
    gate_grad, up_grad, down_grad = call(
        functools.partial(wgrad_body, half, len(waves)),
        [sds((1, quarter, half), BF16), sds((1, quarter, half), BF16), sds((1, half, quarter), BF16)], 0,
        (*[rows[w] for w in waves], *[full[w] for w in waves]),
    )
    return (token_grad, gate_grad, up_grad, down_grad)


def solution(mesh):
    placed = (
        P(("expert", "replica"), "seq"),
        P(("expert", "replica"), "seq"),
        P(("expert", "replica")),
        P(("expert", "replica"), None),
        P("expert", "seq", "replica"),
        P("expert", "seq", "replica"),
        P("expert", "replica", "seq"),
    )
    return jax.shard_map(
        steps,
        mesh=mesh,
        in_specs=placed,
        out_specs=(
            P(("expert", "replica"), "seq"),
            P("expert", "seq", "replica"),
            P("expert", "seq", "replica"),
            P("expert", "replica", "seq"),
        ),
        check_vma=False,
    )
```

```python
import functools

import jax
import jax.numpy as jnp
from jax import lax
from jax.experimental import pallas as pl
from jax.experimental.pallas import tpu as pltpu
from jax.sharding import PartitionSpec as P


F32 = jnp.float32
BF16 = jnp.bfloat16
VMEM = pltpu.VMEM


def mm(left, right, dims):
    return lax.dot_general(left, right, (dims, ((), ())), preferred_element_type=F32)


NN = ((1,), (0,))
NT = ((1,), (1,))
TN = ((0,), (0,))


def vm(x):
    return pltpu.with_memory_space_constraint(x, pltpu.VMEM)


def hbm(x):
    return pltpu.with_memory_space_constraint(x, pltpu.HBM)


def call(body, outs, args, raw=()):
    return pl.pallas_call(
        body,
        out_shape=outs,
        in_specs=[pl.BlockSpec(memory_space=VMEM)] * len(args),
        out_specs=jax.tree.map(lambda _: pl.BlockSpec(memory_space=VMEM), outs),
        compiler_params=pltpu.CompilerParams(vmem_limit_bytes=12 << 20),
    )(*[hbm(a) if i in raw else vm(a) for i, a in enumerate(args)])


def column(row):
    count = row.shape[1]
    eye = lax.broadcasted_iota(jnp.int32, (count, count), 0) == lax.broadcasted_iota(jnp.int32, (count, count), 1)
    return jnp.sum(jnp.where(eye, row, jnp.zeros_like(row)), axis=1, keepdims=True)


def ranks(ids):
    count = ids.shape[0]
    lanes = lax.broadcasted_iota(jnp.int32, (count, 128), 1)
    onehot = jnp.where(ids == lanes, 1.0, 0.0)
    lower = jnp.where(
        lax.broadcasted_iota(jnp.int32, (count, count), 0) > lax.broadcasted_iota(jnp.int32, (count, count), 1), 1.0, 0.0
    )
    before = mm(lower.astype(BF16), onehot.astype(BF16), NN)
    return jnp.sum(before * onehot, axis=1, keepdims=True).astype(jnp.int32)


def slots(ids, rank, owner, cap):
    places = lax.broadcasted_iota(jnp.int32, (ids.shape[0], cap), 1)
    return jnp.where((ids == owner) & (rank == places), 1.0, 0.0).astype(BF16)


def send_body(n_expert, cap, ids_ref, rw_ref, tokens_ref, cot_ref, *outs):
    ids = column(ids_ref[...])
    rank = ranks(ids)
    tokens = tokens_ref[...]
    scaled = (column(rw_ref[...]) * cot_ref[...].astype(F32)).astype(BF16)
    for k in range(n_expert):
        pick = slots(ids, rank, lax.axis_index("expert") ^ k, cap)
        outs[k][0, 0] = mm(pick, tokens, TN).astype(BF16)
        outs[k][0, 1] = mm(pick, scaled, TN).astype(BF16)


def side(refs, which):
    return jnp.concatenate([r[j, which] for r in refs for j in range(r.shape[0])], axis=0)


def part_body(half, n, *refs):
    rows, (wg_ref, wu_ref, wd_ref), outs = refs[:n], refs[n:n + 3], refs[n + 3:]
    x, g = side(rows, 0), side(rows, 1)
    parts = (mm(x, wg_ref[...], NN), mm(x, wu_ref[...], NN), mm(g, wd_ref[...], NT))
    size = outs[0].shape[0]
    for i in range(n):
        for j in range(3):
            outs[i][:, j * half:(j + 1) * half] = parts[j][i * size:(i + 1) * size].astype(BF16)


def at_edge():
    z = lax.axis_index("seq")
    return (z == 0) | (z == 3)


def join_body(now, old, *refs):
    came_ref = refs[0]
    if now:
        part_ref, pair_ref = refs[1], refs[-1 - old]
        pair_ref[...] = (part_ref[...].astype(F32) + came_ref[...].astype(F32)).astype(BF16)
    if old:
        act_ref, full_ref = refs[1 + now], refs[-1]

        @pl.when(at_edge())
        def _():
            full_ref[...] = came_ref[...]

        @pl.when(jnp.logical_not(at_edge()))
        def _():
            full_ref[...] = act_ref[...]


def act_body(half, mixed, s_ref, m_ref, *refs):
    o_ref = refs[mixed]
    gate = s_ref[:, :half].astype(F32) + m_ref[:, :half].astype(F32)
    upper = s_ref[:, half:2 * half].astype(F32) + m_ref[:, half:2 * half].astype(F32)
    hgrad = s_ref[:, 2 * half:].astype(F32) + m_ref[:, 2 * half:].astype(F32)
    sigma = jax.nn.sigmoid(gate)
    active = gate * sigma
    o_ref[:, :half] = (hgrad * upper * sigma * (1.0 + gate * (1.0 - sigma))).astype(BF16)
    o_ref[:, half:2 * half] = (hgrad * active).astype(BF16)
    o_ref[:, 2 * half:] = (active * upper).astype(BF16)
    if mixed:
        part_ref, send_ref = refs[0], refs[2]

        @pl.when(at_edge())
        def _():
            send_ref[...] = part_ref[...]

        @pl.when(jnp.logical_not(at_edge()))
        def _():
            send_ref[...] = o_ref[...]


def out_body(half, n, *refs):
    acts, (wg_ref, wu_ref, o_ref) = refs[:n], refs[n:]
    a = jnp.concatenate([r[:, :2 * half] for r in acts], axis=0)
    o_ref[...] = (mm(a[:, :half], wg_ref[...], NT) + mm(a[:, half:], wu_ref[...], NT)).astype(BF16)


def total_body(start, mine_ref, *refs):
    o_ref = refs[-1]
    value = mine_ref[start:start + o_ref.shape[0]].astype(F32)
    for r in refs[:-1]:
        value = value + r[...].astype(F32)
    o_ref[...] = value.astype(BF16)


def wgrad_body(half, n, last, *refs):
    rows, acts, rest = refs[:n], refs[n:2 * n], refs[2 * n:]
    x, g = side(rows, 0), side(rows, 1)
    a = jnp.concatenate([r[...] for r in acts], axis=0)
    gx, gd = mm(x, a[:, :2 * half], TN), mm(a[:, 2 * half:], g, TN)
    if last:
        px_ref, pd_ref, gg_ref, gu_ref, gd_ref = rest
        gg_ref[0] = (px_ref[:, :half] + gx[:, :half]).astype(BF16)
        gu_ref[0] = (px_ref[:, half:] + gx[:, half:]).astype(BF16)
        gd_ref[0] = (pd_ref[...] + gd).astype(BF16)
    else:
        rest[0][...] = gx
        rest[1][...] = gd


def final_body(n_expert, cap, ids_ref, rw_ref, *refs):
    ids = column(ids_ref[...])
    rank = ranks(ids)
    total = None
    for k in range(n_expert):
        term = mm(slots(ids, rank, lax.axis_index("expert") ^ k, cap), refs[k][...], NN)
        total = term if total is None else total + term
    refs[n_expert][...] = (column(rw_ref[...]) * total).astype(BF16)


def steps(tokens, cotangent, route_weight, expert_ids, gate_weight, up_weight, down_weight):
    n_expert = lax.axis_size("expert")
    n_rep = lax.axis_size("replica")
    n_seq = lax.axis_size("seq")
    assert n_seq == 4 and n_expert % 4 == 0
    count, quarter = tokens.shape
    half = gate_weight.shape[2]
    cap = -(-(3 * count // (2 * n_expert)) // 8) * 8
    each = n_expert // 4
    w_gate, w_up, w_down = gate_weight[0], up_weight[0], down_weight[0]
    rw = route_weight.reshape(1, count)
    ids = expert_ids.reshape(1, count)
    keep = lambda *shape: pltpu.VMEM(shape, BF16)

    def swap(x, axis, k):
        return lax.ppermute(x, axis, [(i, i ^ k) for i in range(lax.axis_size(axis))])

    send = call(
        functools.partial(send_body, n_expert, cap), [keep(1, 2, cap, quarter)] * n_expert,
        (ids, rw, tokens, cotangent), (0, 1, 2, 3),
    )
    got = [send[0]] + [swap(send[k], "expert", k) for k in range(1, n_expert)]
    rows = {}
    for j in range(4):
        blocks = got[j * each:(j + 1) * each]
        rows[0, j] = blocks[0] if each == 1 else jnp.concatenate(blocks, axis=0)
    for q in range(1, n_rep):
        for j in range(4):
            rows[q, j] = swap(rows[0, j], "replica", q)
    size = each * cap
    parts = {}
    for q in range(n_rep):
        for pair in ((0, 1), (2, 3)):
            done = call(
                functools.partial(part_body, half, 2), [keep(size, 3 * half)] * 2,
                (*[rows[q, j] for j in pair], w_gate, w_up, w_down),
                (2, 3, 4) if (q, pair) == (0, (0, 1)) else (),
            )
            parts[q, pair[0]], parts[q, pair[1]] = done

    waves = [(0, 1), (0, 2), (0, 3)]
    waves += [(q, j) for q in range(1, n_rep) for j in (2, 3, 1, 0)] + [(0, 0)]
    lag = 3
    inward, outward, middle = [(0, 1), (3, 2)], [(1, 0), (2, 3)], [(1, 2), (2, 1)]
    acts, full = {}, {}
    leaving = {i: parts[waves[i]] for i in range(lag)}
    wave = keep(size, 3 * half)
    for i in range(len(waves) + lag):
        now = waves[i] if i < len(waves) else None
        old = waves[i - lag] if i >= lag else None
        pairs = (inward if now else []) + (outward if old else [])
        came = lax.ppermute(leaving[i], "seq", pairs)
        done = call(
            functools.partial(join_body, int(now is not None), int(old is not None)),
            [wave] * ((now is not None) + (old is not None)),
            (came, *([parts[now]] if now else []), *([acts[old]] if old else [])),
        )
        if old is not None:
            full[old] = done[-1]
        if now is not None:
            following = [parts[waves[i + lag]]] if i + lag < len(waves) else []
            both = call(
                functools.partial(act_body, half, len(following)), [wave] * (1 + len(following)),
                (done[0], lax.ppermute(done[0], "seq", middle), *following),
            )
            acts[now], leaving[i + lag] = both[0], both[-1]

    def out(q, js):
        return call(
            functools.partial(out_body, half, len(js)), keep(len(js) * size, quarter),
            (*[full[q, j] for j in js], w_gate, w_up),
        )

    mine = {}
    for js in ((2, 3), (1,), (0,)):
        rows_of = out(0, js)
        for n, j in enumerate(js):
            mine[j] = (n, rows_of)
    total = {}
    for j in range(4):
        back = [swap(out(q, (j,)), "replica", q) for q in range(1, n_rep)]
        n, rows_of = mine[j]
        total[j] = call(functools.partial(total_body, n * size), keep(size, quarter), (rows_of, *back))
    ret = [total[k // each][k % each * cap:(k % each + 1) * cap] for k in range(n_expert)]
    ret = [ret[0]] + [swap(ret[k], "expert", k) for k in range(1, n_expert)]
    sds = jax.ShapeDtypeStruct
    token_grad = call(functools.partial(final_body, n_expert, cap), sds((count, quarter), BF16), (ids, rw, *ret))
    early, late = waves[:-2], waves[-2:]
    part_x, part_d = call(
        functools.partial(wgrad_body, half, len(early), False),
        [pltpu.VMEM((quarter, 2 * half), F32), pltpu.VMEM((half, quarter), F32)],
        (*[rows[w] for w in early], *[full[w] for w in early]),
    )
    gate_grad, up_grad, down_grad = call(
        functools.partial(wgrad_body, half, len(late), True),
        [sds((1, quarter, half), BF16), sds((1, quarter, half), BF16), sds((1, half, quarter), BF16)],
        (*[rows[w] for w in late], *[full[w] for w in late], part_x, part_d),
    )
    return (token_grad, gate_grad, up_grad, down_grad)


def solution(mesh):
    placed = (
        P(("expert", "replica"), "seq"),
        P(("expert", "replica"), "seq"),
        P(("expert", "replica")),
        P(("expert", "replica"), None),
        P("expert", "seq", "replica"),
        P("expert", "seq", "replica"),
        P("expert", "replica", "seq"),
    )
    return jax.shard_map(
        steps,
        mesh=mesh,
        in_specs=placed,
        out_specs=(
            P(("expert", "replica"), "seq"),
            P("expert", "seq", "replica"),
            P("expert", "seq", "replica"),
            P("expert", "replica", "seq"),
        ),
        check_vma=False,
    )
```

```python
import functools

import jax
import jax.numpy as jnp
from jax import lax
from jax.experimental import pallas as pl
from jax.experimental.pallas import tpu as pltpu
from jax.sharding import PartitionSpec as P


F32 = jnp.float32
BF16 = jnp.bfloat16
VMEM = pltpu.VMEM


def mm(left, right, dims):
    return lax.dot_general(left, right, (dims, ((), ())), preferred_element_type=F32)


NN = ((1,), (0,))
NT = ((1,), (1,))
TN = ((0,), (0,))


def vm(x):
    return pltpu.with_memory_space_constraint(x, pltpu.VMEM)


def hbm(x):
    return pltpu.with_memory_space_constraint(x, pltpu.HBM)


def call(body, outs, args, raw=()):
    return pl.pallas_call(
        body,
        out_shape=outs,
        in_specs=[pl.BlockSpec(memory_space=VMEM)] * len(args),
        out_specs=jax.tree.map(lambda _: pl.BlockSpec(memory_space=VMEM), outs),
        compiler_params=pltpu.CompilerParams(vmem_limit_bytes=12 << 20),
    )(*[hbm(a) if i in raw else vm(a) for i, a in enumerate(args)])


def column(row):
    count = row.shape[1]
    eye = lax.broadcasted_iota(jnp.int32, (count, count), 0) == lax.broadcasted_iota(jnp.int32, (count, count), 1)
    return jnp.sum(jnp.where(eye, row, jnp.zeros_like(row)), axis=1, keepdims=True)


def ranks(ids):
    count = ids.shape[0]
    lanes = lax.broadcasted_iota(jnp.int32, (count, 128), 1)
    onehot = jnp.where(ids == lanes, 1.0, 0.0)
    lower = jnp.where(
        lax.broadcasted_iota(jnp.int32, (count, count), 0) > lax.broadcasted_iota(jnp.int32, (count, count), 1), 1.0, 0.0
    )
    before = mm(lower.astype(BF16), onehot.astype(BF16), NN)
    return jnp.sum(before * onehot, axis=1, keepdims=True).astype(jnp.int32)


def slots(ids, rank, owner, cap):
    places = lax.broadcasted_iota(jnp.int32, (ids.shape[0], cap), 1)
    return jnp.where((ids == owner) & (rank == places), 1.0, 0.0).astype(BF16)


def send_body(n_expert, cap, ids_ref, rw_ref, tokens_ref, cot_ref, *outs):
    ids = column(ids_ref[...])
    rank = ranks(ids)
    tokens = tokens_ref[...]
    scaled = (column(rw_ref[...]) * cot_ref[...].astype(F32)).astype(BF16)
    for k in range(n_expert):
        pick = slots(ids, rank, lax.axis_index("expert") ^ k, cap)
        outs[n_expert][k] = pick
        outs[k][0, 0] = mm(pick, tokens, TN).astype(BF16)
        outs[k][0, 1] = mm(pick, scaled, TN).astype(BF16)


def side(refs, which):
    return jnp.concatenate([r[j, which] for r in refs for j in range(r.shape[0])], axis=0)


def part_body(half, n, *refs):
    rows, (wg_ref, wu_ref, wd_ref), outs = refs[:n], refs[n:n + 3], refs[n + 3:]
    x, g = side(rows, 0), side(rows, 1)
    parts = (mm(x, wg_ref[...], NN), mm(x, wu_ref[...], NN), mm(g, wd_ref[...], NT))
    size = outs[0].shape[0]
    for i in range(n):
        for j in range(3):
            outs[i][:, j * half:(j + 1) * half] = parts[j][i * size:(i + 1) * size].astype(BF16)


def at_edge():
    z = lax.axis_index("seq")
    return (z == 0) | (z == 3)


def join_body(now, old, *refs):
    came_ref = refs[0]
    if now:
        part_ref, pair_ref = refs[1], refs[-1 - old]
        pair_ref[...] = (part_ref[...].astype(F32) + came_ref[...].astype(F32)).astype(BF16)
    if old:
        act_ref, full_ref = refs[1 + now], refs[-1]

        @pl.when(at_edge())
        def _():
            full_ref[...] = came_ref[...]

        @pl.when(jnp.logical_not(at_edge()))
        def _():
            full_ref[...] = act_ref[...]


def act_body(half, mixed, s_ref, m_ref, *refs):
    o_ref = refs[mixed]
    gate = s_ref[:, :half].astype(F32) + m_ref[:, :half].astype(F32)
    upper = s_ref[:, half:2 * half].astype(F32) + m_ref[:, half:2 * half].astype(F32)
    hgrad = s_ref[:, 2 * half:].astype(F32) + m_ref[:, 2 * half:].astype(F32)
    sigma = jax.nn.sigmoid(gate)
    active = gate * sigma
    o_ref[:, :half] = (hgrad * upper * sigma * (1.0 + gate * (1.0 - sigma))).astype(BF16)
    o_ref[:, half:2 * half] = (hgrad * active).astype(BF16)
    o_ref[:, 2 * half:] = (active * upper).astype(BF16)
    if mixed:
        part_ref, send_ref = refs[0], refs[2]

        @pl.when(at_edge())
        def _():
            send_ref[...] = part_ref[...]

        @pl.when(jnp.logical_not(at_edge()))
        def _():
            send_ref[...] = o_ref[...]


def out_body(half, n, *refs):
    acts, (wg_ref, wu_ref), outs = refs[:n], refs[n:n + 2], refs[n + 2:]
    a = jnp.concatenate([r[:, :2 * half] for r in acts], axis=0)
    o = (mm(a[:, :half], wg_ref[...], NT) + mm(a[:, half:], wu_ref[...], NT)).astype(BF16)
    size = o.shape[0] // n
    for i in range(n):
        outs[i][...] = o[i * size:(i + 1) * size]


def total_body(*refs):
    value = refs[0][...].astype(F32)
    for r in refs[1:-1]:
        value = value + r[...].astype(F32)
    refs[-1][...] = value.astype(BF16)


def wgrad_body(half, n, last, *refs):
    rows, acts, rest = refs[:n], refs[n:2 * n], refs[2 * n:]
    x, g = side(rows, 0), side(rows, 1)
    a = jnp.concatenate([r[...] for r in acts], axis=0)
    gx, gd = mm(x, a[:, :2 * half], TN), mm(a[:, 2 * half:], g, TN)
    if last:
        px_ref, pd_ref, gg_ref, gu_ref, gd_ref = rest
        gg_ref[0] = (px_ref[:, :half] + gx[:, :half]).astype(BF16)
        gu_ref[0] = (px_ref[:, half:] + gx[:, half:]).astype(BF16)
        gd_ref[0] = (pd_ref[...] + gd).astype(BF16)
    else:
        rest[0][...] = gx
        rest[1][...] = gd


def final_body(n_expert, rw_ref, pick_ref, *refs):
    total = None
    for k in range(n_expert):
        term = mm(pick_ref[k], refs[k][...], NN)
        total = term if total is None else total + term
    refs[n_expert][...] = (column(rw_ref[...]) * total).astype(BF16)


def steps(tokens, cotangent, route_weight, expert_ids, gate_weight, up_weight, down_weight):
    n_expert = lax.axis_size("expert")
    n_rep = lax.axis_size("replica")
    n_seq = lax.axis_size("seq")
    assert n_seq == 4 and n_expert % 4 == 0
    count, quarter = tokens.shape
    half = gate_weight.shape[2]
    cap = -(-(3 * count // (2 * n_expert)) // 8) * 8
    each = n_expert // 4
    w_gate, w_up, w_down = gate_weight[0], up_weight[0], down_weight[0]
    rw = route_weight.reshape(1, count)
    ids = expert_ids.reshape(1, count)
    keep = lambda *shape: pltpu.VMEM(shape, BF16)

    def swap(x, axis, k):
        return lax.ppermute(x, axis, [(i, i ^ k) for i in range(lax.axis_size(axis))])

    send = call(
        functools.partial(send_body, n_expert, cap), [keep(1, 2, cap, quarter)] * n_expert + [keep(n_expert, count, cap)],
        (ids, rw, tokens, cotangent), (0, 1, 2, 3),
    )
    got = [send[0]] + [swap(send[k], "expert", k) for k in range(1, n_expert)]
    rows = {}
    for j in range(4):
        blocks = got[j * each:(j + 1) * each]
        rows[0, j] = blocks[0] if each == 1 else jnp.concatenate(blocks, axis=0)
    for q in range(1, n_rep):
        for j in range(4):
            rows[q, j] = swap(rows[0, j], "replica", q)
    size = each * cap
    parts = {}
    for q in range(n_rep):
        for js in ((0, 1), (2, 3)) if q == 0 else ((0,), (1,), (2,), (3,)):
            done = call(
                functools.partial(part_body, half, len(js)), [keep(size, 3 * half)] * len(js),
                (*[rows[q, j] for j in js], w_gate, w_up, w_down),
                (2, 3, 4) if (q, js[0]) == (0, 0) else (),
            )
            for n, j in enumerate(js):
                parts[q, j] = done[n]

    waves = [(0, 1)] + [(q, j) for j in range(4) for q in range(1, n_rep)] + [(0, 2), (0, 3), (0, 0)]
    lag = 3
    inward, outward, middle = [(0, 1), (3, 2)], [(1, 0), (2, 3)], [(1, 2), (2, 1)]
    acts, full = {}, {}
    leaving = {i: parts[waves[i]] for i in range(lag)}
    wave = keep(size, 3 * half)
    for i in range(len(waves) + lag):
        now = waves[i] if i < len(waves) else None
        old = waves[i - lag] if i >= lag else None
        pairs = (inward if now else []) + (outward if old else [])
        came = lax.ppermute(leaving[i], "seq", pairs)
        done = call(
            functools.partial(join_body, int(now is not None), int(old is not None)),
            [wave] * ((now is not None) + (old is not None)),
            (came, *([parts[now]] if now else []), *([acts[old]] if old else [])),
        )
        if old is not None:
            full[old] = done[-1]
        if now is not None:
            following = [parts[waves[i + lag]]] if i + lag < len(waves) else []
            both = call(
                functools.partial(act_body, half, len(following)), [wave] * (1 + len(following)),
                (done[0], lax.ppermute(done[0], "seq", middle), *following),
            )
            acts[now], leaving[i + lag] = both[0], both[-1]

    groups = [[(0, 1)] + [(q, 0) for q in range(1, n_rep)]]
    groups += [[(q, j)] for j in range(1, 4) for q in range(1, n_rep)] + [[(0, 2)], [(0, 3)], [(0, 0)]]
    outs = {}
    for group in groups:
        done = call(
            functools.partial(out_body, half, len(group)), [keep(size, quarter)] * len(group),
            (*[full[w] for w in group], w_gate, w_up),
        )
        outs.update(zip(group, done))
    total = {}
    for j in range(4):
        back = [swap(outs[q, j], "replica", q) for q in range(1, n_rep)]
        total[j] = call(total_body, keep(size, quarter), (outs[0, j], *back))
    ret = [total[k // each][k % each * cap:(k % each + 1) * cap] for k in range(n_expert)]
    ret = [ret[0]] + [swap(ret[k], "expert", k) for k in range(1, n_expert)]
    sds = jax.ShapeDtypeStruct
    token_grad = call(functools.partial(final_body, n_expert), sds((count, quarter), BF16), (rw, send[n_expert], *ret))
    early, late = waves[:-2], waves[-2:]
    part_x, part_d = call(
        functools.partial(wgrad_body, half, len(early), False),
        [pltpu.VMEM((quarter, 2 * half), F32), pltpu.VMEM((half, quarter), F32)],
        (*[rows[w] for w in early], *[full[w] for w in early]),
    )
    gate_grad, up_grad, down_grad = call(
        functools.partial(wgrad_body, half, len(late), True),
        [sds((1, quarter, half), BF16), sds((1, quarter, half), BF16), sds((1, half, quarter), BF16)],
        (*[rows[w] for w in late], *[full[w] for w in late], part_x, part_d),
    )
    return (token_grad, gate_grad, up_grad, down_grad)


def solution(mesh):
    placed = (
        P(("expert", "replica"), "seq"),
        P(("expert", "replica"), "seq"),
        P(("expert", "replica")),
        P(("expert", "replica"), None),
        P("expert", "seq", "replica"),
        P("expert", "seq", "replica"),
        P("expert", "replica", "seq"),
    )
    return jax.shard_map(
        steps,
        mesh=mesh,
        in_specs=placed,
        out_specs=(
            P(("expert", "replica"), "seq"),
            P("expert", "seq", "replica"),
            P("expert", "seq", "replica"),
            P("expert", "replica", "seq"),
        ),
        check_vma=False,
    )
```

```python
import functools

import jax
import jax.numpy as jnp
from jax import lax
from jax.experimental import pallas as pl
from jax.experimental.pallas import tpu as pltpu
from jax.sharding import PartitionSpec as P


F32 = jnp.float32
BF16 = jnp.bfloat16
VMEM = pltpu.VMEM


def mm(left, right, dims):
    return lax.dot_general(left, right, (dims, ((), ())), preferred_element_type=F32)


NN = ((1,), (0,))
NT = ((1,), (1,))
TN = ((0,), (0,))


def vm(x):
    return pltpu.with_memory_space_constraint(x, pltpu.VMEM)


def hbm(x):
    return pltpu.with_memory_space_constraint(x, pltpu.HBM)


def call(body, outs, args, raw=()):
    return pl.pallas_call(
        body,
        out_shape=outs,
        in_specs=[pl.BlockSpec(memory_space=VMEM)] * len(args),
        out_specs=jax.tree.map(lambda _: pl.BlockSpec(memory_space=VMEM), outs),
        compiler_params=pltpu.CompilerParams(vmem_limit_bytes=12 << 20),
    )(*[hbm(a) if i in raw else vm(a) for i, a in enumerate(args)])


def column(row):
    count = row.shape[1]
    eye = lax.broadcasted_iota(jnp.int32, (count, count), 0) == lax.broadcasted_iota(jnp.int32, (count, count), 1)
    return jnp.sum(jnp.where(eye, row, jnp.zeros_like(row)), axis=1, keepdims=True)


def ranks(ids, n_expert):
    count = ids.shape[1]
    onehot = jnp.where(lax.broadcasted_iota(jnp.int32, (max(n_expert, 16), count), 0) == ids, 1.0, 0.0)
    upper = jnp.where(
        lax.broadcasted_iota(jnp.int32, (count, count), 0) < lax.broadcasted_iota(jnp.int32, (count, count), 1), 1.0, 0.0
    )
    before = mm(onehot.astype(BF16), upper.astype(BF16), NN)
    return jnp.sum(before * onehot, axis=0, keepdims=True).astype(jnp.int32)


def send_body(n_expert, cap, ids_ref, rw_ref, tokens_ref, cot_ref, *outs):
    ids, rw = ids_ref[...], rw_ref[...]
    rank = ranks(ids, n_expert)
    places = lax.broadcasted_iota(jnp.int32, (cap, ids.shape[1]), 0)
    for k in range(n_expert):
        here = (ids == lax.axis_index("expert") ^ k) & (rank == places)
        pick = jnp.where(here, 1.0, 0.0).astype(BF16)
        weight = jnp.sum(jnp.where(here, rw, 0.0), axis=1, keepdims=True)
        outs[n_expert][k] = pick
        outs[k][0, 0] = mm(pick, tokens_ref[...], NN).astype(BF16)
        outs[k][0, 1] = (weight * mm(pick, cot_ref[...], NN)).astype(BF16)


def side(refs, which):
    return jnp.concatenate([r[j, which] for r in refs for j in range(r.shape[0])], axis=0)


def part_body(half, n, *refs):
    rows, (wg_ref, wu_ref, wd_ref), outs = refs[:n], refs[n:n + 3], refs[n + 3:]
    x, g = side(rows, 0), side(rows, 1)
    parts = (mm(x, wg_ref[...], NN), mm(x, wu_ref[...], NN), mm(g, wd_ref[...], NT))
    size = outs[0].shape[0]
    for i in range(n):
        for j in range(3):
            outs[i][:, j * half:(j + 1) * half] = parts[j][i * size:(i + 1) * size].astype(BF16)


def at_edge():
    z = lax.axis_index("seq")
    return (z == 0) | (z == 3)


def join_body(now, old, *refs):
    came_ref = refs[0]
    if now:
        part_ref, pair_ref = refs[1], refs[-1 - old]
        pair_ref[...] = (part_ref[...].astype(F32) + came_ref[...].astype(F32)).astype(BF16)
    if old:
        act_ref, full_ref = refs[1 + now], refs[-1]

        @pl.when(at_edge())
        def _():
            full_ref[...] = came_ref[...]

        @pl.when(jnp.logical_not(at_edge()))
        def _():
            full_ref[...] = act_ref[...]


def act_body(half, mixed, s_ref, m_ref, *refs):
    o_ref = refs[mixed]
    gate = s_ref[:, :half].astype(F32) + m_ref[:, :half].astype(F32)
    upper = s_ref[:, half:2 * half].astype(F32) + m_ref[:, half:2 * half].astype(F32)
    hgrad = s_ref[:, 2 * half:].astype(F32) + m_ref[:, 2 * half:].astype(F32)
    sigma = jax.nn.sigmoid(gate)
    active = gate * sigma
    o_ref[:, :half] = (hgrad * upper * sigma * (1.0 + gate * (1.0 - sigma))).astype(BF16)
    o_ref[:, half:2 * half] = (hgrad * active).astype(BF16)
    o_ref[:, 2 * half:] = (active * upper).astype(BF16)
    if mixed:
        part_ref, send_ref = refs[0], refs[2]

        @pl.when(at_edge())
        def _():
            send_ref[...] = part_ref[...]

        @pl.when(jnp.logical_not(at_edge()))
        def _():
            send_ref[...] = o_ref[...]


def out_body(half, n, *refs):
    acts, (wg_ref, wu_ref), outs = refs[:n], refs[n:n + 2], refs[n + 2:]
    a = jnp.concatenate([r[:, :2 * half] for r in acts], axis=0)
    o = (mm(a[:, :half], wg_ref[...], NT) + mm(a[:, half:], wu_ref[...], NT)).astype(BF16)
    size = o.shape[0] // n
    for i in range(n):
        outs[i][...] = o[i * size:(i + 1) * size]


def total_body(*refs):
    value = refs[0][...].astype(F32)
    for r in refs[1:-1]:
        value = value + r[...].astype(F32)
    refs[-1][...] = value.astype(BF16)


def wgrad_body(half, n, last, *refs):
    rows, acts, rest = refs[:n], refs[n:2 * n], refs[2 * n:]
    x, g = side(rows, 0), side(rows, 1)
    a = jnp.concatenate([r[...] for r in acts], axis=0)
    gx, gd = mm(x, a[:, :2 * half], TN), mm(a[:, 2 * half:], g, TN)
    if last:
        px_ref, pd_ref, gg_ref, gu_ref, gd_ref = rest
        gg_ref[0] = (px_ref[:, :half] + gx[:, :half]).astype(BF16)
        gu_ref[0] = (px_ref[:, half:] + gx[:, half:]).astype(BF16)
        gd_ref[0] = (pd_ref[...] + gd).astype(BF16)
    else:
        rest[0][...] = gx
        rest[1][...] = gd


def final_body(n_expert, rw_ref, pick_ref, *refs):
    total = None
    for k in range(n_expert):
        term = mm(pick_ref[k], refs[k][...], TN)
        total = term if total is None else total + term
    refs[n_expert][...] = (column(rw_ref[...]) * total).astype(BF16)


def steps(tokens, cotangent, route_weight, expert_ids, gate_weight, up_weight, down_weight):
    n_expert = lax.axis_size("expert")
    n_rep = lax.axis_size("replica")
    n_seq = lax.axis_size("seq")
    assert n_seq == 4 and n_expert % 4 == 0
    count, quarter = tokens.shape
    half = gate_weight.shape[2]
    cap = -(-(3 * count // (2 * n_expert)) // 8) * 8
    each = n_expert // 4
    w_gate, w_up, w_down = gate_weight[0], up_weight[0], down_weight[0]
    rw = route_weight.reshape(1, count)
    ids = expert_ids.reshape(1, count)
    keep = lambda *shape: pltpu.VMEM(shape, BF16)

    def swap(x, axis, k):
        return lax.ppermute(x, axis, [(i, i ^ k) for i in range(lax.axis_size(axis))])

    send = call(
        functools.partial(send_body, n_expert, cap), [keep(1, 2, cap, quarter)] * n_expert + [keep(n_expert, cap, count)],
        (ids, rw, tokens, cotangent), (0, 1, 2, 3),
    )
    got = [send[0]] + [swap(send[k], "expert", k) for k in range(1, n_expert)]
    rows = {}
    for j in range(4):
        blocks = got[j * each:(j + 1) * each]
        rows[0, j] = blocks[0] if each == 1 else jnp.concatenate(blocks, axis=0)
    for q in range(1, n_rep):
        for j in range(4):
            rows[q, j] = swap(rows[0, j], "replica", q)
    size = each * cap
    parts = {}
    for q in range(n_rep):
        for js in ((0, 1), (2, 3)) if q == 0 else ((0,), (1,), (2,), (3,)):
            done = call(
                functools.partial(part_body, half, len(js)), [keep(size, 3 * half)] * len(js),
                (*[rows[q, j] for j in js], w_gate, w_up, w_down),
                (2, 3, 4) if (q, js[0]) == (0, 0) else (),
            )
            for n, j in enumerate(js):
                parts[q, j] = done[n]

    waves = [(0, 1)] + [(q, j) for j in range(4) for q in range(1, n_rep)] + [(0, 2), (0, 3), (0, 0)]
    lag = 3
    inward, outward, middle = [(0, 1), (3, 2)], [(1, 0), (2, 3)], [(1, 2), (2, 1)]
    acts, full = {}, {}
    leaving = {i: parts[waves[i]] for i in range(lag)}
    wave = keep(size, 3 * half)
    for i in range(len(waves) + lag):
        now = waves[i] if i < len(waves) else None
        old = waves[i - lag] if i >= lag else None
        pairs = (inward if now else []) + (outward if old else [])
        came = lax.ppermute(leaving[i], "seq", pairs)
        done = call(
            functools.partial(join_body, int(now is not None), int(old is not None)),
            [wave] * ((now is not None) + (old is not None)),
            (came, *([parts[now]] if now else []), *([acts[old]] if old else [])),
        )
        if old is not None:
            full[old] = done[-1]
        if now is not None:
            following = [parts[waves[i + lag]]] if i + lag < len(waves) else []
            both = call(
                functools.partial(act_body, half, len(following)), [wave] * (1 + len(following)),
                (done[0], lax.ppermute(done[0], "seq", middle), *following),
            )
            acts[now], leaving[i + lag] = both[0], both[-1]

    groups = [[(0, 1)] + [(q, 0) for q in range(1, n_rep)]]
    groups += [[(q, j)] for j in range(1, 4) for q in range(1, n_rep)] + [[(0, 2)], [(0, 3)], [(0, 0)]]
    outs = {}
    for group in groups:
        done = call(
            functools.partial(out_body, half, len(group)), [keep(size, quarter)] * len(group),
            (*[full[w] for w in group], w_gate, w_up),
        )
        outs.update(zip(group, done))
    total = {}
    for j in range(4):
        back = [swap(outs[q, j], "replica", q) for q in range(1, n_rep)]
        total[j] = call(total_body, keep(size, quarter), (outs[0, j], *back))
    ret = [total[k // each][k % each * cap:(k % each + 1) * cap] for k in range(n_expert)]
    ret = [ret[0]] + [swap(ret[k], "expert", k) for k in range(1, n_expert)]
    sds = jax.ShapeDtypeStruct
    token_grad = call(functools.partial(final_body, n_expert), sds((count, quarter), BF16), (rw, send[n_expert], *ret))
    early, late = waves[:-2], waves[-2:]
    part_x, part_d = call(
        functools.partial(wgrad_body, half, len(early), False),
        [pltpu.VMEM((quarter, 2 * half), F32), pltpu.VMEM((half, quarter), F32)],
        (*[rows[w] for w in early], *[full[w] for w in early]),
    )
    gate_grad, up_grad, down_grad = call(
        functools.partial(wgrad_body, half, len(late), True),
        [sds((1, quarter, half), BF16), sds((1, quarter, half), BF16), sds((1, half, quarter), BF16)],
        (*[rows[w] for w in late], *[full[w] for w in late], part_x, part_d),
    )
    return (token_grad, gate_grad, up_grad, down_grad)


def solution(mesh):
    placed = (
        P(("expert", "replica"), "seq"),
        P(("expert", "replica"), "seq"),
        P(("expert", "replica")),
        P(("expert", "replica"), None),
        P("expert", "seq", "replica"),
        P("expert", "seq", "replica"),
        P("expert", "replica", "seq"),
    )
    return jax.shard_map(
        steps,
        mesh=mesh,
        in_specs=placed,
        out_specs=(
            P(("expert", "replica"), "seq"),
            P("expert", "seq", "replica"),
            P("expert", "seq", "replica"),
            P("expert", "replica", "seq"),
        ),
        check_vma=False,
    )
```

```python
import functools

import jax
import jax.numpy as jnp
from jax import lax
from jax.experimental import pallas as pl
from jax.experimental.pallas import tpu as pltpu
from jax.sharding import PartitionSpec as P


F32 = jnp.float32
BF16 = jnp.bfloat16
VMEM = pltpu.VMEM


def mm(left, right, dims):
    return lax.dot_general(left, right, (dims, ((), ())), preferred_element_type=F32)


NN = ((1,), (0,))
NT = ((1,), (1,))
TN = ((0,), (0,))


def vm(x):
    return pltpu.with_memory_space_constraint(x, pltpu.VMEM)


def hbm(x):
    return pltpu.with_memory_space_constraint(x, pltpu.HBM)


def call(body, outs, args, raw=()):
    return pl.pallas_call(
        body,
        out_shape=outs,
        in_specs=[pl.BlockSpec(memory_space=VMEM)] * len(args),
        out_specs=jax.tree.map(lambda _: pl.BlockSpec(memory_space=VMEM), outs),
        compiler_params=pltpu.CompilerParams(vmem_limit_bytes=12 << 20),
    )(*[hbm(a) if i in raw else vm(a) for i, a in enumerate(args)])


def column(row):
    count = row.shape[1]
    eye = lax.broadcasted_iota(jnp.int32, (count, count), 0) == lax.broadcasted_iota(jnp.int32, (count, count), 1)
    return jnp.sum(jnp.where(eye, row, jnp.zeros_like(row)), axis=1, keepdims=True)


def ranks(ids, n_expert):
    count = ids.shape[1]
    onehot = jnp.where(lax.broadcasted_iota(jnp.int32, (max(n_expert, 16), count), 0) == ids, 1.0, 0.0)
    upper = jnp.where(
        lax.broadcasted_iota(jnp.int32, (count, count), 0) < lax.broadcasted_iota(jnp.int32, (count, count), 1), 1.0, 0.0
    )
    before = mm(onehot.astype(BF16), upper.astype(BF16), NN)
    return jnp.sum(before * onehot, axis=0, keepdims=True).astype(jnp.int32)


def send_body(n_expert, cap, ids_ref, rw_ref, tokens_ref, cot_ref, *outs):
    ids, rw = ids_ref[...], rw_ref[...]
    rank = ranks(ids, n_expert)
    places = lax.broadcasted_iota(jnp.int32, (cap, ids.shape[1]), 0)
    for k in range(n_expert):
        here = (ids == lax.axis_index("expert") ^ k) & (rank == places)
        pick = jnp.where(here, 1.0, 0.0).astype(BF16)
        weight = jnp.sum(jnp.where(here, rw, 0.0), axis=1, keepdims=True)
        outs[n_expert][k] = pick
        outs[k][0, 0] = mm(pick, tokens_ref[...], NN).astype(BF16)
        outs[k][0, 1] = (weight * mm(pick, cot_ref[...], NN)).astype(BF16)


def side(refs, which):
    return jnp.concatenate([r[j, which] for r in refs for j in range(r.shape[0])], axis=0)


def part_body(half, n, *refs):
    rows, (wg_ref, wu_ref, wd_ref), outs = refs[:n], refs[n:n + 3], refs[n + 3:]
    x, g = side(rows, 0), side(rows, 1)
    parts = (mm(x, wg_ref[...], NN), mm(x, wu_ref[...], NN), mm(g, wd_ref[...], NT))
    size = outs[0].shape[0]
    for i in range(n):
        for j in range(3):
            outs[i][:, j * half:(j + 1) * half] = parts[j][i * size:(i + 1) * size].astype(BF16)


def at_edge():
    z = lax.axis_index("seq")
    return (z == 0) | (z == 3)


def join_body(now, old, *refs):
    came_ref = refs[0]
    if now:
        part_ref, pair_ref = refs[1], refs[-1 - old]
        pair_ref[...] = (part_ref[...].astype(F32) + came_ref[...].astype(F32)).astype(BF16)
    if old:
        act_ref, full_ref = refs[1 + now], refs[-1]

        @pl.when(at_edge())
        def _():
            full_ref[...] = came_ref[...]

        @pl.when(jnp.logical_not(at_edge()))
        def _():
            full_ref[...] = act_ref[...]


def act_body(half, mixed, s_ref, m_ref, *refs):
    o_ref = refs[mixed]
    gate = s_ref[:, :half].astype(F32) + m_ref[:, :half].astype(F32)
    upper = s_ref[:, half:2 * half].astype(F32) + m_ref[:, half:2 * half].astype(F32)
    hgrad = s_ref[:, 2 * half:].astype(F32) + m_ref[:, 2 * half:].astype(F32)
    sigma = jax.nn.sigmoid(gate)
    active = gate * sigma
    o_ref[:, :half] = (hgrad * upper * sigma * (1.0 + gate * (1.0 - sigma))).astype(BF16)
    o_ref[:, half:2 * half] = (hgrad * active).astype(BF16)
    o_ref[:, 2 * half:] = (active * upper).astype(BF16)
    if mixed:
        part_ref, send_ref = refs[0], refs[2]

        @pl.when(at_edge())
        def _():
            send_ref[...] = part_ref[...]

        @pl.when(jnp.logical_not(at_edge()))
        def _():
            send_ref[...] = o_ref[...]


def out_body(half, n, *refs):
    acts, (wg_ref, wu_ref), outs = refs[:n], refs[n:n + 2], refs[n + 2:]
    a = jnp.concatenate([r[:, :2 * half] for r in acts], axis=0)
    o = (mm(a[:, :half], wg_ref[...], NT) + mm(a[:, half:], wu_ref[...], NT)).astype(BF16)
    size = outs[0].shape[0]
    for i in range(len(outs)):
        outs[i][...] = o[i * size:(i + 1) * size]


def total_body(n, *refs):
    value = refs[0][...].astype(F32)
    size = value.shape[0]
    for r in refs[1:-1]:
        value = value + r[n * size:(n + 1) * size].astype(F32)
    refs[-1][...] = value.astype(BF16)


def wgrad_body(half, n, last, *refs):
    rows, acts, rest = refs[:n], refs[n:2 * n], refs[2 * n:]
    x, g = side(rows, 0), side(rows, 1)
    a = jnp.concatenate([r[...] for r in acts], axis=0)
    gx, gd = mm(x, a[:, :2 * half], TN), mm(a[:, 2 * half:], g, TN)
    if last:
        px_ref, pd_ref, gg_ref, gu_ref, gd_ref = rest
        gg_ref[0] = (px_ref[:, :half] + gx[:, :half]).astype(BF16)
        gu_ref[0] = (px_ref[:, half:] + gx[:, half:]).astype(BF16)
        gd_ref[0] = (pd_ref[...] + gd).astype(BF16)
    else:
        rest[0][...] = gx
        rest[1][...] = gd


def final_body(n_expert, rw_ref, pick_ref, *refs):
    total = None
    for k in range(n_expert):
        term = mm(pick_ref[k], refs[k][...], TN)
        total = term if total is None else total + term
    refs[n_expert][...] = (column(rw_ref[...]) * total).astype(BF16)


def steps(tokens, cotangent, route_weight, expert_ids, gate_weight, up_weight, down_weight):
    n_expert = lax.axis_size("expert")
    n_rep = lax.axis_size("replica")
    n_seq = lax.axis_size("seq")
    assert n_seq == 4 and n_expert % 4 == 0
    count, quarter = tokens.shape
    half = gate_weight.shape[2]
    cap = -(-(3 * count // (2 * n_expert)) // 8) * 8
    each = n_expert // 4
    w_gate, w_up, w_down = gate_weight[0], up_weight[0], down_weight[0]
    rw = route_weight.reshape(1, count)
    ids = expert_ids.reshape(1, count)
    keep = lambda *shape: pltpu.VMEM(shape, BF16)

    def swap(x, axis, k):
        return lax.ppermute(x, axis, [(i, i ^ k) for i in range(lax.axis_size(axis))])

    send = call(
        functools.partial(send_body, n_expert, cap), [keep(1, 2, cap, quarter)] * n_expert + [keep(n_expert, cap, count)],
        (ids, rw, tokens, cotangent), (0, 1, 2, 3),
    )
    got = [send[0]] + [swap(send[k], "expert", k) for k in range(1, n_expert)]
    rows = {}
    for j in range(4):
        blocks = got[j * each:(j + 1) * each]
        rows[0, j] = blocks[0] if each == 1 else jnp.concatenate(blocks, axis=0)
    for q in range(1, n_rep):
        for j in range(4):
            rows[q, j] = swap(rows[0, j], "replica", q)
    size = each * cap
    parts = {}
    for q in range(n_rep):
        for js in ((0, 1), (2, 3)) if q == 0 else ((0,), (1,), (2,), (3,)):
            done = call(
                functools.partial(part_body, half, len(js)), [keep(size, 3 * half)] * len(js),
                (*[rows[q, j] for j in js], w_gate, w_up, w_down),
                (2, 3, 4) if (q, js[0]) == (0, 0) else (),
            )
            for n, j in enumerate(js):
                parts[q, j] = done[n]

    waves = [(0, 1)] + [(q, j) for j in range(4) for q in range(1, n_rep)] + [(0, 2), (0, 3), (0, 0)]
    lag = 3
    inward, outward, middle = [(0, 1), (3, 2)], [(1, 0), (2, 3)], [(1, 2), (2, 1)]
    acts, full = {}, {}
    leaving = {i: parts[waves[i]] for i in range(lag)}
    wave = keep(size, 3 * half)
    for i in range(len(waves) + lag):
        now = waves[i] if i < len(waves) else None
        old = waves[i - lag] if i >= lag else None
        pairs = (inward if now else []) + (outward if old else [])
        came = lax.ppermute(leaving[i], "seq", pairs)
        done = call(
            functools.partial(join_body, int(now is not None), int(old is not None)),
            [wave] * ((now is not None) + (old is not None)),
            (came, *([parts[now]] if now else []), *([acts[old]] if old else [])),
        )
        if old is not None:
            full[old] = done[-1]
        if now is not None:
            following = [parts[waves[i + lag]]] if i + lag < len(waves) else []
            both = call(
                functools.partial(act_body, half, len(following)), [wave] * (1 + len(following)),
                (done[0], lax.ppermute(done[0], "seq", middle), *following),
            )
            acts[now], leaving[i + lag] = both[0], both[-1]

    def out(group, whole=False):
        shape = [keep(len(group) * size, quarter)] if whole else [keep(size, quarter)] * len(group)
        return call(functools.partial(out_body, half, len(group)), shape, (*[full[w] for w in group], w_gate, w_up))

    back = {0: [], 2: []}
    for j in (0, 2):
        for q in range(1, n_rep):
            both = out([(q, j), (q, j + 1)], True)[0]
            back[j].append(swap(both, "replica", q))
    mine = dict(zip((1, 2, 3), out([(0, 1), (0, 2), (0, 3)])))
    mine[0] = out([(0, 0)])[0]
    total = {}
    for j in range(4):
        total[j] = call(functools.partial(total_body, j % 2), keep(size, quarter), (mine[j], *back[j - j % 2]))
    ret = [total[k // each][k % each * cap:(k % each + 1) * cap] for k in range(n_expert)]
    ret = [ret[0]] + [swap(ret[k], "expert", k) for k in range(1, n_expert)]
    sds = jax.ShapeDtypeStruct
    token_grad = call(functools.partial(final_body, n_expert), sds((count, quarter), BF16), (rw, send[n_expert], *ret))
    early, late = waves[:-2], waves[-2:]
    part_x, part_d = call(
        functools.partial(wgrad_body, half, len(early), False),
        [pltpu.VMEM((quarter, 2 * half), F32), pltpu.VMEM((half, quarter), F32)],
        (*[rows[w] for w in early], *[full[w] for w in early]),
    )
    gate_grad, up_grad, down_grad = call(
        functools.partial(wgrad_body, half, len(late), True),
        [sds((1, quarter, half), BF16), sds((1, quarter, half), BF16), sds((1, half, quarter), BF16)],
        (*[rows[w] for w in late], *[full[w] for w in late], part_x, part_d),
    )
    return (token_grad, gate_grad, up_grad, down_grad)


def solution(mesh):
    placed = (
        P(("expert", "replica"), "seq"),
        P(("expert", "replica"), "seq"),
        P(("expert", "replica")),
        P(("expert", "replica"), None),
        P("expert", "seq", "replica"),
        P("expert", "seq", "replica"),
        P("expert", "replica", "seq"),
    )
    return jax.shard_map(
        steps,
        mesh=mesh,
        in_specs=placed,
        out_specs=(
            P(("expert", "replica"), "seq"),
            P("expert", "seq", "replica"),
            P("expert", "seq", "replica"),
            P("expert", "replica", "seq"),
        ),
        check_vma=False,
    )
```
